128 devices in a mesh: row: 16 (over x, z), col: 8 (over y, core).
Axes of the slice: x: 4, y: 4, z: 4, core: 2. Of those that a mesh axis runs over, the one named last changes fastest.
Arguments:
- tokens: bfloat16 [384, 8192], P('col', 'row'), may hold values from -6 to 6
- gate_weight: bfloat16 [8192, 26624], P('row', 'col'), may hold values from -0.09375 to 0.09375
- up_weight: bfloat16 [8192, 26624], P('row', 'col'), may hold values from -0.09375 to 0.09375
- down_weight: bfloat16 [26624, 8192], P('col', 'row'), may hold values from -0.0546875 to 0.0546875
- gate_mask: int32 [64, 208], P('row', 'col'), may hold values from 0 to 1, as said below
- up_mask: int32 [64, 208], P('row', 'col'), may hold values from 0 to 1, as said below
- down_mask: int32 [208, 64], P('col', 'row'), may hold values from 0 to 1, as said below
- out_grad: bfloat16 [384, 8192], P('col', 'row'), may hold values from -6 to 6
Outputs:
- mixed_out: bfloat16 [384, 8192], P('col', 'row')
- grad_gate: bfloat16 [8192, 26624], P('row', 'col')
- grad_up: bfloat16 [8192, 26624], P('row', 'col')
- grad_down: bfloat16 [26624, 8192], P('col', 'row')
- input_grad: bfloat16 [384, 8192], P('col', 'row')
The draws below stay inside these ranges and needn't reach their ends.
Inputs may be any that keep to these rules, and one draw needn't show every extreme that they name: `gate_mask`: 1 keeps a tile of 128 x 128 weights, 0 drops it; the share kept differs between rows of tiles. `up_mask`: 1 keeps a tile of 128 x 128 weights, 0 drops it; the share kept differs between rows of tiles. `down_mask`: 1 keeps a tile of 128 x 128 weights, 0 drops it; the share kept differs between columns of tiles.
All inputs are finite; a program needn't handle non-finite values.
Results may differ from the reference program's by a relative error of at most 0.0049.
Values may be sent and summed in bfloat16 or wider, within the bound.
A program may use at most 128 MiB of HBM per device.

```python
import jax
import jax.numpy as jnp

D = 8192
FF = 26624
TILE = 128
TOKENS = 384


def uneven_mask(key, outer, inner):
    limits = jax.random.randint(jax.random.fold_in(key, 11), (outer, 1), 250, 751)
    values = jax.random.randint(jax.random.fold_in(key, 12), (outer, inner), 0, 1000)
    return (values < limits).astype(jnp.int32)


def draw_gate_mask(key, part):
    return uneven_mask(jax.random.fold_in(key, 1), D // TILE, FF // TILE)


def draw_up_mask(key, part):
    return uneven_mask(jax.random.fold_in(key, 2), D // TILE, FF // TILE)


def draw_down_mask(key, part):
    return uneven_mask(jax.random.fold_in(key, 3), D // TILE, FF // TILE).T


def block_scale(rng, shape, pieces, least, top_value):
    loudness = 1.0
    for dim, blocks in pieces:
        heights = jax.random.uniform(jax.random.fold_in(jax.random.fold_in(rng, 6), dim), (blocks,), jnp.float32, least / len(pieces), top_value / len(pieces))
        loudness = loudness * jnp.repeat(jnp.exp(heights), shape[dim] // blocks).reshape((-1,) + (1,) * (len(shape) - 1 - dim))
    return loudness


def gaussian(own_key, extent, spread, bound, split=(), held_as=jnp.bfloat16):
    result = jax.random.normal(own_key, extent, jnp.float32) * spread
    if len(split) > 0:
        result = block_scale(own_key, extent, split, -0.22, 0.18) * result
    return jnp.clip(result, min=-bound, max=bound).astype(held_as)


def setup_inputs(seed: int = 0) -> dict:
    key_list = jax.random.split(jax.random.key(seed), 9)
    return {
        "tokens": gaussian(key_list[0], (TOKENS, D), 1.0, 6.0, ((0, 8), (1, 16))),
        "gate_weight": gaussian(key_list[1], (D, FF), (D // 2) ** -0.5, 0.09375, ((0, 16), (1, 8))),
        "up_weight": gaussian(key_list[2], (D, FF), (D // 2) ** -0.5, 0.09375, ((0, 16), (1, 8))),
        "down_weight": gaussian(key_list[3], (FF, D), (FF // 2) ** -0.5, 0.0546875, ((0, 8), (1, 16))),
        "gate_mask": draw_gate_mask(jax.random.fold_in(key_list[8], 71), 0),
        "up_mask": draw_up_mask(jax.random.fold_in(key_list[8], 71), 0),
        "down_mask": draw_down_mask(jax.random.fold_in(key_list[8], 71), 0),
        "out_grad": gaussian(key_list[7], (TOKENS, D), 1.0, 6.0, ((0, 8), (1, 16))),
    }


def masked(weight, mask):
    rows_w, cols_w = weight.shape
    blocks = weight.reshape(rows_w // TILE, TILE, cols_w // TILE, TILE)
    kept = mask.astype(weight.dtype)[:, None, :, None]
    return (blocks * kept).reshape(rows_w, cols_w)


def reference(tokens, gate_weight, up_weight, down_weight, gate_mask, up_mask, down_mask, out_grad):
    gate_full = masked(gate_weight, gate_mask)
    up_full = masked(up_weight, up_mask)
    down_full = masked(down_weight, down_mask)
    gate_val = jnp.dot(tokens, gate_full, preferred_element_type=jnp.float32)
    up_val = jnp.dot(tokens, up_full, preferred_element_type=jnp.float32)
    sigmoid_gate = jax.nn.sigmoid(gate_val)
    silu_gate = gate_val * sigmoid_gate
    hidden = (silu_gate * up_val).astype(jnp.bfloat16)
    mixed_out = jnp.dot(hidden, down_full, preferred_element_type=jnp.float32).astype(jnp.bfloat16)
    hidden_grad = jnp.dot(out_grad, down_full.T, preferred_element_type=jnp.float32)
    gate_grad = (hidden_grad * up_val * sigmoid_gate * (1.0 + gate_val * (1.0 - sigmoid_gate))).astype(jnp.bfloat16)
    up_grad = (hidden_grad * silu_gate).astype(jnp.bfloat16)
    grad_gate = masked(jnp.dot(tokens.T, gate_grad, preferred_element_type=jnp.float32), gate_mask).astype(jnp.bfloat16)
    grad_up = masked(jnp.dot(tokens.T, up_grad, preferred_element_type=jnp.float32), up_mask).astype(jnp.bfloat16)
    grad_down = masked(jnp.dot(hidden.T, out_grad, preferred_element_type=jnp.float32), down_mask).astype(jnp.bfloat16)
    input_grad = (jnp.dot(gate_grad, gate_full.T, preferred_element_type=jnp.float32)
                  + jnp.dot(up_grad, up_full.T, preferred_element_type=jnp.float32)).astype(jnp.bfloat16)
    return (mixed_out, grad_gate, grad_up, grad_down, input_grad)
```

```python
import jax
import jax.numpy as jnp
from jax import lax
from jax.sharding import PartitionSpec as P


def expand(weight, mask):
    rows_w, cols_w = weight.shape
    tile_size = rows_w // mask.shape[0]
    blocks = weight.reshape(mask.shape[0], tile_size, mask.shape[1], tile_size)
    kept = mask.astype(weight.dtype)[:, None, :, None]
    return (blocks * kept).reshape(rows_w, cols_w)


def contract_last(left, right):
    return lax.dot_general(
        left, right, (((1,), (1,)), ((), ())), preferred_element_type=jnp.float32
    )


def contract_first(left, right):
    return lax.dot_general(
        left, right, (((0,), (0,)), ((), ())), preferred_element_type=jnp.float32
    )


def body(tokens, gate_weight, up_weight, down_weight, gate_mask, up_mask, down_mask, out_grad):
    feat = tokens.shape[1]
    both_all = lax.all_gather(
        jnp.concatenate([tokens, out_grad], axis=1), "col", axis=0, tiled=True
    )
    tok_all = both_all[:, :feat]
    grad_all = both_all[:, feat:]
    w_gate = expand(gate_weight, gate_mask)
    w_up = expand(up_weight, up_mask)
    w_down = expand(down_weight, down_mask)

    gate_mine = lax.psum_scatter(
        jnp.dot(tok_all, w_gate, preferred_element_type=jnp.float32),
        "row", scatter_dimension=0, tiled=True,
    )
    up_mine = lax.psum_scatter(
        jnp.dot(tok_all, w_up, preferred_element_type=jnp.float32),
        "row", scatter_dimension=0, tiled=True,
    )
    sigmoid_gate = jax.nn.sigmoid(gate_mine)
    silu_gate = gate_mine * sigmoid_gate
    hidden_mine = (silu_gate * up_mine).astype(jnp.bfloat16)
    hidden_all = lax.all_gather(hidden_mine, "row", axis=0, tiled=True)

    hidden_grad = lax.psum_scatter(
        contract_last(grad_all, w_down), "row", scatter_dimension=0, tiled=True
    )
    gate_grad = (
        hidden_grad * up_mine * sigmoid_gate * (1.0 + gate_mine * (1.0 - sigmoid_gate))
    ).astype(jnp.bfloat16)
    up_grad = (hidden_grad * silu_gate).astype(jnp.bfloat16)
    grad_pair = lax.all_gather(
        jnp.concatenate([gate_grad, up_grad], axis=1), "row", axis=0, tiled=True
    )
    half_width = gate_weight.shape[1]
    weight_pair = contract_first(tok_all, grad_pair)
    grad_gate = expand(weight_pair[:, :half_width], gate_mask).astype(jnp.bfloat16)
    grad_up = expand(weight_pair[:, half_width:], up_mask).astype(jnp.bfloat16)
    grad_down = expand(contract_first(hidden_all, grad_all), down_mask).astype(jnp.bfloat16)

    mixed_part = jnp.dot(hidden_all, w_down, preferred_element_type=jnp.float32)
    input_part = contract_last(grad_pair[:, :half_width], w_gate) + contract_last(
        grad_pair[:, half_width:], w_up
    )
    out_sums = lax.psum_scatter(
        jnp.concatenate([mixed_part, input_part], axis=1), "col", scatter_dimension=0, tiled=True
    )
    mixed_out = out_sums[:, :feat].astype(jnp.bfloat16)
    input_grad = out_sums[:, feat:].astype(jnp.bfloat16)
    return (mixed_out, grad_gate, grad_up, grad_down, input_grad)


def solution(mesh):
    in_specs = (
        P("col", "row"),
        P("row", "col"),
        P("row", "col"),
        P("col", "row"),
        P("row", "col"),
        P("row", "col"),
        P("col", "row"),
        P("col", "row"),
    )
    out_specs = (
        P("col", "row"),
        P("row", "col"),
        P("row", "col"),
        P("col", "row"),
        P("col", "row"),
    )
    return jax.shard_map(body, mesh=mesh, in_specs=in_specs, out_specs=out_specs, check_vma=False)
```

```python
import jax
import jax.numpy as jnp
from jax import lax
from jax.sharding import PartitionSpec as P

CHUNKS = 2


def expand(weight, mask):
    rows_w, cols_w = weight.shape
    tile_size = rows_w // mask.shape[0]
    blocks = weight.reshape(mask.shape[0], tile_size, mask.shape[1], tile_size)
    kept = mask.astype(weight.dtype)[:, None, :, None]
    return (blocks * kept).reshape(rows_w, cols_w)


def contract_last(left, right):
    return lax.dot_general(
        left, right, (((1,), (1,)), ((), ())), preferred_element_type=jnp.float32
    )


def contract_first(left, right):
    return lax.dot_general(
        left, right, (((0,), (0,)), ((), ())), preferred_element_type=jnp.float32
    )


def body(tokens, gate_weight, up_weight, down_weight, gate_mask, up_mask, down_mask, out_grad):
    feat = tokens.shape[1]
    both_all = lax.all_gather(
        jnp.concatenate([tokens, out_grad], axis=1), "col", axis=0, tiled=True
    )
    tok_all = both_all[:, :feat]
    grad_all = both_all[:, feat:]
    width = gate_weight.shape[1]
    tile = width // gate_mask.shape[1]
    tiles = gate_mask.shape[1]
    bounds = [tiles * k // CHUNKS for k in range(CHUNKS + 1)]

    gate_parts, up_parts, down_parts = [], [], []
    mixed_part = None
    input_part = None
    prev_sums = None
    for k in range(CHUNKS):
        t0, t1 = bounds[k], bounds[k + 1]
        h0, h1 = t0 * tile, t1 * tile
        g_mask = gate_mask[:, t0:t1]
        u_mask = up_mask[:, t0:t1]
        d_mask = down_mask[t0:t1, :]
        w_gate = expand(gate_weight[:, h0:h1], g_mask)
        w_up = expand(up_weight[:, h0:h1], u_mask)
        w_down = expand(down_weight[h0:h1, :], d_mask)
        n = h1 - h0
        partial = jnp.concatenate(
            [
                jnp.dot(tok_all, w_gate, preferred_element_type=jnp.float32),
                jnp.dot(tok_all, w_up, preferred_element_type=jnp.float32),
                contract_last(grad_all, w_down),
            ],
            axis=1,
        )
        if prev_sums is not None:
            partial, _ = lax.optimization_barrier((partial, prev_sums))
        sums = lax.psum(partial, "row")
        prev_sums = sums
        gate_val = sums[:, :n]
        up_val = sums[:, n : 2 * n]
        hidden_grad = sums[:, 2 * n :]
        sigmoid_gate = jax.nn.sigmoid(gate_val)
        silu_gate = gate_val * sigmoid_gate
        hidden = (silu_gate * up_val).astype(jnp.bfloat16)
        gate_grad = (
            hidden_grad * up_val * sigmoid_gate * (1.0 + gate_val * (1.0 - sigmoid_gate))
        ).astype(jnp.bfloat16)
        up_grad = (hidden_grad * silu_gate).astype(jnp.bfloat16)
        gate_parts.append(expand(contract_first(tok_all, gate_grad), g_mask).astype(jnp.bfloat16))
        up_parts.append(expand(contract_first(tok_all, up_grad), u_mask).astype(jnp.bfloat16))
        down_parts.append(expand(contract_first(hidden, grad_all), d_mask).astype(jnp.bfloat16))
        m = jnp.dot(hidden, w_down, preferred_element_type=jnp.float32)
        i = contract_last(gate_grad, w_gate) + contract_last(up_grad, w_up)
        mixed_part = m if mixed_part is None else mixed_part + m
        input_part = i if input_part is None else input_part + i

    out_sums = lax.psum_scatter(
        jnp.concatenate([mixed_part, input_part], axis=1), "col", scatter_dimension=0, tiled=True
    )
    mixed_out = out_sums[:, :feat].astype(jnp.bfloat16)
    input_grad = out_sums[:, feat:].astype(jnp.bfloat16)
    grad_gate = jnp.concatenate(gate_parts, axis=1)
    grad_up = jnp.concatenate(up_parts, axis=1)
    grad_down = jnp.concatenate(down_parts, axis=0)
    return (mixed_out, grad_gate, grad_up, grad_down, input_grad)


def solution(mesh):
    in_specs = (
        P("col", "row"),
        P("row", "col"),
        P("row", "col"),
        P("col", "row"),
        P("row", "col"),
        P("row", "col"),
        P("col", "row"),
        P("col", "row"),
    )
    out_specs = (
        P("col", "row"),
        P("row", "col"),
        P("row", "col"),
        P("col", "row"),
        P("col", "row"),
    )
    return jax.shard_map(body, mesh=mesh, in_specs=in_specs, out_specs=out_specs, check_vma=False)
```

```python
import jax
import jax.numpy as jnp
from jax import lax
from jax.sharding import PartitionSpec as P

CHUNKS = 1


def expand(weight, mask):
    rows_w, cols_w = weight.shape
    tile_size = rows_w // mask.shape[0]
    blocks = weight.reshape(mask.shape[0], tile_size, mask.shape[1], tile_size)
    kept = mask.astype(weight.dtype)[:, None, :, None]
    return (blocks * kept).reshape(rows_w, cols_w)


def expand_flat(values, mask):
    rows_v, cols_v = values.shape
    rep_r = rows_v // mask.shape[0]
    rep_c = cols_v // mask.shape[1]
    kept = jnp.repeat(jnp.repeat(mask.astype(values.dtype), rep_r, axis=0), rep_c, axis=1)
    return values * kept


def contract_last(left, right):
    return lax.dot_general(
        left, right, (((1,), (1,)), ((), ())), preferred_element_type=jnp.float32
    )


def contract_first(left, right):
    return lax.dot_general(
        left, right, (((0,), (0,)), ((), ())), preferred_element_type=jnp.float32
    )


def body(tokens, gate_weight, up_weight, down_weight, gate_mask, up_mask, down_mask, out_grad):
    feat = tokens.shape[1]
    both_all = lax.all_gather(
        jnp.concatenate([tokens, out_grad], axis=1), "col", axis=0, tiled=True
    )
    tok_all = both_all[:, :feat]
    grad_all = both_all[:, feat:]
    width = gate_weight.shape[1]
    tile = width // gate_mask.shape[1]
    tiles = gate_mask.shape[1]
    bounds = [tiles * k // CHUNKS for k in range(CHUNKS + 1)]

    gate_parts, up_parts, down_parts = [], [], []
    mixed_part = None
    input_part = None
    prev_sums = None
    for k in range(CHUNKS):
        t0, t1 = bounds[k], bounds[k + 1]
        h0, h1 = t0 * tile, t1 * tile
        g_mask = gate_mask[:, t0:t1]
        u_mask = up_mask[:, t0:t1]
        d_mask = down_mask[t0:t1, :]
        w_gate = expand(gate_weight[:, h0:h1], g_mask)
        w_up = expand(up_weight[:, h0:h1], u_mask)
        w_down = expand(down_weight[h0:h1, :], d_mask)
        n = h1 - h0
        partial = jnp.concatenate(
            [
                jnp.dot(tok_all, w_gate, preferred_element_type=jnp.float32),
                jnp.dot(tok_all, w_up, preferred_element_type=jnp.float32),
                contract_last(grad_all, w_down),
            ],
            axis=1,
        )
        if prev_sums is not None:
            partial, _ = lax.optimization_barrier((partial, prev_sums))
        sums = lax.psum(partial, "row")
        prev_sums = sums
        gate_val = sums[:, :n]
        up_val = sums[:, n : 2 * n]
        hidden_grad = sums[:, 2 * n :]
        sigmoid_gate = jax.nn.sigmoid(gate_val)
        silu_gate = gate_val * sigmoid_gate
        hidden = (silu_gate * up_val).astype(jnp.bfloat16)
        gate_grad = (
            hidden_grad * up_val * sigmoid_gate * (1.0 + gate_val * (1.0 - sigmoid_gate))
        ).astype(jnp.bfloat16)
        up_grad = (hidden_grad * silu_gate).astype(jnp.bfloat16)
        gate_parts.append(expand_flat(contract_first(tok_all, gate_grad), g_mask).astype(jnp.bfloat16))
        up_parts.append(expand_flat(contract_first(tok_all, up_grad), u_mask).astype(jnp.bfloat16))
        down_parts.append(expand_flat(contract_first(hidden, grad_all), d_mask).astype(jnp.bfloat16))
        m = jnp.dot(hidden, w_down, preferred_element_type=jnp.float32)
        i = contract_last(gate_grad, w_gate) + contract_last(up_grad, w_up)
        mixed_part = m if mixed_part is None else mixed_part + m
        input_part = i if input_part is None else input_part + i

    out_sums = lax.psum_scatter(
        jnp.concatenate([mixed_part, input_part], axis=1), "col", scatter_dimension=0, tiled=True
    )
    mixed_out = out_sums[:, :feat].astype(jnp.bfloat16)
    input_grad = out_sums[:, feat:].astype(jnp.bfloat16)
    grad_gate = jnp.concatenate(gate_parts, axis=1)
    grad_up = jnp.concatenate(up_parts, axis=1)
    grad_down = jnp.concatenate(down_parts, axis=0)
    return (mixed_out, grad_gate, grad_up, grad_down, input_grad)


def solution(mesh):
    in_specs = (
        P("col", "row"),
        P("row", "col"),
        P("row", "col"),
        P("col", "row"),
        P("row", "col"),
        P("row", "col"),
        P("col", "row"),
        P("col", "row"),
    )
    out_specs = (
        P("col", "row"),
        P("row", "col"),
        P("row", "col"),
        P("col", "row"),
        P("col", "row"),
    )
    return jax.shard_map(body, mesh=mesh, in_specs=in_specs, out_specs=out_specs, check_vma=False)
```

```python
import jax
import jax.numpy as jnp
from jax import lax
from jax.sharding import PartitionSpec as P

CHUNKS = 1


def expand(weight, mask):
    rows_w, cols_w = weight.shape
    tile_size = rows_w // mask.shape[0]
    blocks = weight.reshape(mask.shape[0], tile_size, mask.shape[1], tile_size)
    kept = mask.astype(weight.dtype)[:, None, :, None]
    return (blocks * kept).reshape(rows_w, cols_w)


def expand_flat(values, mask):
    rows_v, cols_v = values.shape
    rep_r = rows_v // mask.shape[0]
    rep_c = cols_v // mask.shape[1]
    kept = jnp.repeat(mask.astype(values.dtype), rep_c, axis=1)
    blocks = values.reshape(mask.shape[0], rep_r, cols_v)
    return (blocks * kept[:, None, :]).reshape(rows_v, cols_v)


def contract_last(left, right):
    return lax.dot_general(
        left, right, (((1,), (1,)), ((), ())), preferred_element_type=jnp.float32
    )


def contract_first(left, right):
    return lax.dot_general(
        left, right, (((0,), (0,)), ((), ())), preferred_element_type=jnp.float32
    )


def body(tokens, gate_weight, up_weight, down_weight, gate_mask, up_mask, down_mask, out_grad):
    feat = tokens.shape[1]
    both_all = lax.all_gather(
        jnp.concatenate([tokens, out_grad], axis=1), "col", axis=0, tiled=True
    )
    tok_all = both_all[:, :feat]
    grad_all = both_all[:, feat:]
    width = gate_weight.shape[1]
    tile = width // gate_mask.shape[1]
    tiles = gate_mask.shape[1]
    bounds = [tiles * k // CHUNKS for k in range(CHUNKS + 1)]

    gate_parts, up_parts, down_parts = [], [], []
    mixed_part = None
    input_part = None
    prev_sums = None
    for k in range(CHUNKS):
        t0, t1 = bounds[k], bounds[k + 1]
        h0, h1 = t0 * tile, t1 * tile
        g_mask = gate_mask[:, t0:t1]
        u_mask = up_mask[:, t0:t1]
        d_mask = down_mask[t0:t1, :]
        w_gate = expand(gate_weight[:, h0:h1], g_mask)
        w_up = expand(up_weight[:, h0:h1], u_mask)
        w_down = expand(down_weight[h0:h1, :], d_mask)
        n = h1 - h0
        partial = jnp.concatenate(
            [
                jnp.dot(tok_all, w_gate, preferred_element_type=jnp.float32),
                jnp.dot(tok_all, w_up, preferred_element_type=jnp.float32),
                contract_last(grad_all, w_down),
            ],
            axis=1,
        )
        if prev_sums is not None:
            partial, _ = lax.optimization_barrier((partial, prev_sums))
        sums = lax.psum(partial, "row")
        prev_sums = sums
        gate_val = sums[:, :n]
        up_val = sums[:, n : 2 * n]
        hidden_grad = sums[:, 2 * n :]
        sigmoid_gate = jax.nn.sigmoid(gate_val)
        silu_gate = gate_val * sigmoid_gate
        hidden = (silu_gate * up_val).astype(jnp.bfloat16)
        gate_grad = (
            hidden_grad * up_val * sigmoid_gate * (1.0 + gate_val * (1.0 - sigmoid_gate))
        ).astype(jnp.bfloat16)
        up_grad = (hidden_grad * silu_gate).astype(jnp.bfloat16)
        gate_parts.append(expand_flat(contract_first(tok_all, gate_grad), g_mask).astype(jnp.bfloat16))
        up_parts.append(expand_flat(contract_first(tok_all, up_grad), u_mask).astype(jnp.bfloat16))
        down_parts.append(expand_flat(contract_first(hidden, grad_all), d_mask).astype(jnp.bfloat16))
        m = jnp.dot(hidden, w_down, preferred_element_type=jnp.float32)
        i = contract_last(gate_grad, w_gate) + contract_last(up_grad, w_up)
        mixed_part = m if mixed_part is None else mixed_part + m
        input_part = i if input_part is None else input_part + i

    out_sums = lax.psum_scatter(
        jnp.concatenate([mixed_part, input_part], axis=1), "col", scatter_dimension=0, tiled=True
    )
    mixed_out = out_sums[:, :feat].astype(jnp.bfloat16)
    input_grad = out_sums[:, feat:].astype(jnp.bfloat16)
    grad_gate = jnp.concatenate(gate_parts, axis=1)
    grad_up = jnp.concatenate(up_parts, axis=1)
    grad_down = jnp.concatenate(down_parts, axis=0)
    return (mixed_out, grad_gate, grad_up, grad_down, input_grad)


def solution(mesh):
    in_specs = (
        P("col", "row"),
        P("row", "col"),
        P("row", "col"),
        P("col", "row"),
        P("row", "col"),
        P("row", "col"),
        P("col", "row"),
        P("col", "row"),
    )
    out_specs = (
        P("col", "row"),
        P("row", "col"),
        P("row", "col"),
        P("col", "row"),
        P("col", "row"),
    )
    return jax.shard_map(body, mesh=mesh, in_specs=in_specs, out_specs=out_specs, check_vma=False)
```

```python
import jax
import jax.numpy as jnp
from jax import lax
from jax.sharding import PartitionSpec as P

CHUNKS = 1


def expand(weight, mask):
    rows_w, cols_w = weight.shape
    tile_size = rows_w // mask.shape[0]
    blocks = weight.reshape(mask.shape[0], tile_size, mask.shape[1], tile_size)
    kept = mask.astype(weight.dtype)[:, None, :, None]
    return (blocks * kept).reshape(rows_w, cols_w)


def expand_flat(values, mask):
    rows_v, cols_v = values.shape
    rep_r = rows_v // mask.shape[0]
    rep_c = cols_v // mask.shape[1]
    kept = jnp.repeat(mask.astype(values.dtype), rep_c, axis=1)
    blocks = values.reshape(mask.shape[0], rep_r, cols_v)
    return (blocks * kept[:, None, :]).reshape(rows_v, cols_v)


def contract_last(left, right):
    return lax.dot_general(
        left, right, (((1,), (1,)), ((), ())), preferred_element_type=jnp.float32
    )


def contract_first(left, right):
    return lax.dot_general(
        left, right, (((0,), (0,)), ((), ())), preferred_element_type=jnp.float32
    )


def body(tokens, gate_weight, up_weight, down_weight, gate_mask, up_mask, down_mask, out_grad):
    feat = tokens.shape[1]
    both_all = lax.all_gather(
        jnp.concatenate([tokens, out_grad], axis=1), "col", axis=0, tiled=True
    )
    tok_all = both_all[:, :feat]
    grad_all = both_all[:, feat:]
    width = gate_weight.shape[1]
    tile = width // gate_mask.shape[1]
    tiles = gate_mask.shape[1]
    bounds = [tiles * k // CHUNKS for k in range(CHUNKS + 1)]

    gate_parts, up_parts, down_parts = [], [], []
    mixed_part = None
    input_part = None
    prev_sums = None
    for k in range(CHUNKS):
        t0, t1 = bounds[k], bounds[k + 1]
        h0, h1 = t0 * tile, t1 * tile
        g_mask = gate_mask[:, t0:t1]
        u_mask = up_mask[:, t0:t1]
        d_mask = down_mask[t0:t1, :]
        w_gate = expand_flat(gate_weight[:, h0:h1], g_mask)
        w_up = expand_flat(up_weight[:, h0:h1], u_mask)
        w_down = expand_flat(down_weight[h0:h1, :], d_mask)
        n = h1 - h0
        partial = (
            jnp.dot(tok_all, w_gate, preferred_element_type=jnp.float32),
            jnp.dot(tok_all, w_up, preferred_element_type=jnp.float32),
            contract_last(grad_all, w_down),
        )
        if prev_sums is not None:
            partial, _ = lax.optimization_barrier((partial, prev_sums))
        gate_val, up_val, hidden_grad = lax.psum(partial, "row")
        prev_sums = gate_val
        sigmoid_gate = jax.nn.sigmoid(gate_val)
        silu_gate = gate_val * sigmoid_gate
        hidden = (silu_gate * up_val).astype(jnp.bfloat16)
        gate_grad = (
            hidden_grad * up_val * sigmoid_gate * (1.0 + gate_val * (1.0 - sigmoid_gate))
        ).astype(jnp.bfloat16)
        up_grad = (hidden_grad * silu_gate).astype(jnp.bfloat16)
        gate_parts.append(expand_flat(contract_first(tok_all, gate_grad), g_mask).astype(jnp.bfloat16))
        up_parts.append(expand_flat(contract_first(tok_all, up_grad), u_mask).astype(jnp.bfloat16))
        down_parts.append(expand_flat(contract_first(hidden, grad_all), d_mask).astype(jnp.bfloat16))
        m = jnp.dot(hidden, w_down, preferred_element_type=jnp.float32)
        i = contract_last(gate_grad, w_gate) + contract_last(up_grad, w_up)
        mixed_part = m if mixed_part is None else mixed_part + m
        input_part = i if input_part is None else input_part + i

    out_sums = lax.psum_scatter(
        jnp.concatenate([mixed_part, input_part], axis=1), "col", scatter_dimension=0, tiled=True
    )
    mixed_out = out_sums[:, :feat].astype(jnp.bfloat16)
    input_grad = out_sums[:, feat:].astype(jnp.bfloat16)
    grad_gate = jnp.concatenate(gate_parts, axis=1)
    grad_up = jnp.concatenate(up_parts, axis=1)
    grad_down = jnp.concatenate(down_parts, axis=0)
    return (mixed_out, grad_gate, grad_up, grad_down, input_grad)


def solution(mesh):
    in_specs = (
        P("col", "row"),
        P("row", "col"),
        P("row", "col"),
        P("col", "row"),
        P("row", "col"),
        P("row", "col"),
        P("col", "row"),
        P("col", "row"),
    )
    out_specs = (
        P("col", "row"),
        P("row", "col"),
        P("row", "col"),
        P("col", "row"),
        P("col", "row"),
    )
    return jax.shard_map(body, mesh=mesh, in_specs=in_specs, out_specs=out_specs, check_vma=False)
```

```python
import jax
import jax.numpy as jnp
from jax import lax
from jax.sharding import PartitionSpec as P

CHUNKS = 1


def expand(weight, mask):
    rows_w, cols_w = weight.shape
    tile_size = rows_w // mask.shape[0]
    blocks = weight.reshape(mask.shape[0], tile_size, mask.shape[1], tile_size)
    kept = mask.astype(weight.dtype)[:, None, :, None]
    return (blocks * kept).reshape(rows_w, cols_w)


def expand_flat(values, mask):
    rows_v, cols_v = values.shape
    rep_r = rows_v // mask.shape[0]
    rep_c = cols_v // mask.shape[1]
    kept = jnp.repeat(mask.astype(values.dtype), rep_c, axis=1)
    blocks = values.reshape(mask.shape[0], rep_r, cols_v)
    return (blocks * kept[:, None, :]).reshape(rows_v, cols_v)


def contract_last(left, right):
    return lax.dot_general(
        left, right, (((1,), (1,)), ((), ())), preferred_element_type=jnp.float32
    )


def contract_first(left, right):
    return lax.dot_general(
        left, right, (((0,), (0,)), ((), ())), preferred_element_type=jnp.float32
    )


def body(tokens, gate_weight, up_weight, down_weight, gate_mask, up_mask, down_mask, out_grad):
    feat = tokens.shape[1]
    both_all = lax.all_gather(
        jnp.concatenate([tokens, out_grad], axis=1), "col", axis=0, tiled=True
    )
    tok_all = both_all[:, :feat]
    grad_all = both_all[:, feat:]
    width = gate_weight.shape[1]
    tile = width // gate_mask.shape[1]
    tiles = gate_mask.shape[1]
    bounds = [tiles * k // CHUNKS for k in range(CHUNKS + 1)]

    gate_parts, up_parts, down_parts = [], [], []
    mixed_part = None
    input_part = None
    prev_sums = None
    for k in range(CHUNKS):
        t0, t1 = bounds[k], bounds[k + 1]
        h0, h1 = t0 * tile, t1 * tile
        g_mask = gate_mask[:, t0:t1]
        u_mask = up_mask[:, t0:t1]
        d_mask = down_mask[t0:t1, :]
        w_gate = expand_flat(gate_weight[:, h0:h1], g_mask)
        w_up = expand_flat(up_weight[:, h0:h1], u_mask)
        w_down = expand_flat(down_weight[h0:h1, :], d_mask)
        n = h1 - h0
        partial = (
            jnp.dot(tok_all, w_gate, preferred_element_type=jnp.float32),
            jnp.dot(tok_all, w_up, preferred_element_type=jnp.float32),
            contract_last(grad_all, w_down),
        )
        if prev_sums is not None:
            partial, _ = lax.optimization_barrier((partial, prev_sums))
        gate_val, up_val, hidden_grad = lax.psum(partial, "row")
        prev_sums = gate_val

        def activations(gate_val, up_val, hidden_grad):
            sigmoid_gate = jax.nn.sigmoid(gate_val)
            silu_gate = gate_val * sigmoid_gate
            hidden = (silu_gate * up_val).astype(jnp.bfloat16)
            gate_grad = (
                hidden_grad * up_val * sigmoid_gate * (1.0 + gate_val * (1.0 - sigmoid_gate))
            ).astype(jnp.bfloat16)
            up_grad = (hidden_grad * silu_gate).astype(jnp.bfloat16)
            return hidden, gate_grad, up_grad

        hidden, gate_grad, up_grad = activations(gate_val, up_val, hidden_grad)
        m = jnp.dot(hidden, w_down, preferred_element_type=jnp.float32)
        i = contract_last(gate_grad, w_gate) + contract_last(up_grad, w_up)
        hidden, gate_grad, up_grad = activations(
            *lax.optimization_barrier((gate_val, up_val, hidden_grad))
        )
        gate_parts.append(expand_flat(contract_first(tok_all, gate_grad), g_mask).astype(jnp.bfloat16))
        up_parts.append(expand_flat(contract_first(tok_all, up_grad), u_mask).astype(jnp.bfloat16))
        down_parts.append(expand_flat(contract_first(hidden, grad_all), d_mask).astype(jnp.bfloat16))
        mixed_part = m if mixed_part is None else mixed_part + m
        input_part = i if input_part is None else input_part + i

    out_sums = lax.psum_scatter(
        jnp.concatenate([mixed_part, input_part], axis=1), "col", scatter_dimension=0, tiled=True
    )
    mixed_out = out_sums[:, :feat].astype(jnp.bfloat16)
    input_grad = out_sums[:, feat:].astype(jnp.bfloat16)
    grad_gate = jnp.concatenate(gate_parts, axis=1)
    grad_up = jnp.concatenate(up_parts, axis=1)
    grad_down = jnp.concatenate(down_parts, axis=0)
    return (mixed_out, grad_gate, grad_up, grad_down, input_grad)


def solution(mesh):
    in_specs = (
        P("col", "row"),
        P("row", "col"),
        P("row", "col"),
        P("col", "row"),
        P("row", "col"),
        P("row", "col"),
        P("col", "row"),
        P("col", "row"),
    )
    out_specs = (
        P("col", "row"),
        P("row", "col"),
        P("row", "col"),
        P("col", "row"),
        P("col", "row"),
    )
    return jax.shard_map(body, mesh=mesh, in_specs=in_specs, out_specs=out_specs, check_vma=False)
```

```python
import jax
import jax.numpy as jnp
from jax import lax
from jax.sharding import PartitionSpec as P

CHUNKS = 1


def expand(weight, mask):
    rows_w, cols_w = weight.shape
    tile_size = rows_w // mask.shape[0]
    blocks = weight.reshape(mask.shape[0], tile_size, mask.shape[1], tile_size)
    kept = mask.astype(weight.dtype)[:, None, :, None]
    return (blocks * kept).reshape(rows_w, cols_w)


def expand_flat(values, mask):
    rows_v, cols_v = values.shape
    rep_r = rows_v // mask.shape[0]
    rep_c = cols_v // mask.shape[1]
    kept = jnp.repeat(mask.astype(values.dtype), rep_c, axis=1)
    blocks = values.reshape(mask.shape[0], rep_r, cols_v)
    return (blocks * kept[:, None, :]).reshape(rows_v, cols_v)


def contract_last(left, right):
    return lax.dot_general(
        left, right, (((1,), (1,)), ((), ())), preferred_element_type=jnp.float32
    )


def contract_first(left, right):
    return lax.dot_general(
        left, right, (((0,), (0,)), ((), ())), preferred_element_type=jnp.float32
    )


def body(tokens, gate_weight, up_weight, down_weight, gate_mask, up_mask, down_mask, out_grad):
    feat = tokens.shape[1]
    both_all = lax.all_gather(
        jnp.concatenate([tokens, out_grad], axis=1), "col", axis=0, tiled=True
    )
    tok_all = both_all[:, :feat]
    grad_all = both_all[:, feat:]
    width = gate_weight.shape[1]
    tile = width // gate_mask.shape[1]
    tiles = gate_mask.shape[1]
    bounds = [tiles * k // CHUNKS for k in range(CHUNKS + 1)]

    gate_parts, up_parts, down_parts = [], [], []
    mixed_part = None
    input_part = None
    prev_sums = None
    for k in range(CHUNKS):
        t0, t1 = bounds[k], bounds[k + 1]
        h0, h1 = t0 * tile, t1 * tile
        g_mask = gate_mask[:, t0:t1]
        u_mask = up_mask[:, t0:t1]
        d_mask = down_mask[t0:t1, :]
        w_gate = expand_flat(gate_weight[:, h0:h1], g_mask)
        w_up = expand_flat(up_weight[:, h0:h1], u_mask)
        w_down = expand_flat(down_weight[h0:h1, :], d_mask)
        n = h1 - h0
        partial = (
            jnp.dot(tok_all, w_gate, preferred_element_type=jnp.float32),
            jnp.dot(tok_all, w_up, preferred_element_type=jnp.float32),
            contract_last(grad_all, w_down),
        )
        if prev_sums is not None:
            partial, _ = lax.optimization_barrier((partial, prev_sums))
        gate_val, up_val, hidden_grad = lax.psum(partial, "row")
        prev_sums = gate_val
        sigmoid_gate = jax.nn.sigmoid(gate_val)
        silu_gate = gate_val * sigmoid_gate
        hidden = (silu_gate * up_val).astype(jnp.bfloat16)
        gate_grad = (
            hidden_grad * up_val * sigmoid_gate * (1.0 + gate_val * (1.0 - sigmoid_gate))
        ).astype(jnp.bfloat16)
        up_grad = (hidden_grad * silu_gate).astype(jnp.bfloat16)
        gate_parts.append(expand_flat(contract_first(tok_all, gate_grad), g_mask).astype(jnp.bfloat16))
        up_parts.append(expand_flat(contract_first(tok_all, up_grad), u_mask).astype(jnp.bfloat16))
        down_parts.append(expand_flat(contract_first(hidden, grad_all), d_mask).astype(jnp.bfloat16))
        m = jnp.dot(hidden, w_down, preferred_element_type=jnp.float32)
        i = contract_last(gate_grad, w_gate) + contract_last(up_grad, w_up)
        mixed_part = m if mixed_part is None else mixed_part + m
        input_part = i if input_part is None else input_part + i

    both_part = jnp.concatenate([mixed_part, input_part], axis=1)
    ways = lax.axis_size("col")
    spread = lax.all_to_all(both_part, "col", 0, 0, tiled=True)
    out_sums = spread.reshape(ways, spread.shape[0] // ways, spread.shape[1]).sum(axis=0)
    mixed_out = out_sums[:, :feat].astype(jnp.bfloat16)
    input_grad = out_sums[:, feat:].astype(jnp.bfloat16)
    grad_gate = jnp.concatenate(gate_parts, axis=1)
    grad_up = jnp.concatenate(up_parts, axis=1)
    grad_down = jnp.concatenate(down_parts, axis=0)
    return (mixed_out, grad_gate, grad_up, grad_down, input_grad)


def solution(mesh):
    in_specs = (
        P("col", "row"),
        P("row", "col"),
        P("row", "col"),
        P("col", "row"),
        P("row", "col"),
        P("row", "col"),
        P("col", "row"),
        P("col", "row"),
    )
    out_specs = (
        P("col", "row"),
        P("row", "col"),
        P("row", "col"),
        P("col", "row"),
        P("col", "row"),
    )
    return jax.shard_map(body, mesh=mesh, in_specs=in_specs, out_specs=out_specs, check_vma=False)
```

```python
import jax
import jax.numpy as jnp
from jax import lax
from jax.sharding import PartitionSpec as P

CHUNKS = 1


def expand(weight, mask):
    rows_w, cols_w = weight.shape
    tile_size = rows_w // mask.shape[0]
    blocks = weight.reshape(mask.shape[0], tile_size, mask.shape[1], tile_size)
    kept = mask.astype(weight.dtype)[:, None, :, None]
    return (blocks * kept).reshape(rows_w, cols_w)


def expand_flat(values, mask):
    rows_v, cols_v = values.shape
    rep_r = rows_v // mask.shape[0]
    rep_c = cols_v // mask.shape[1]
    kept = jnp.repeat(mask.astype(values.dtype), rep_c, axis=1)
    blocks = values.reshape(mask.shape[0], rep_r, cols_v)
    return (blocks * kept[:, None, :]).reshape(rows_v, cols_v)


def contract_last(left, right):
    return lax.dot_general(
        left, right, (((1,), (1,)), ((), ())), preferred_element_type=jnp.float32
    )


def contract_first(left, right):
    return lax.dot_general(
        left, right, (((0,), (0,)), ((), ())), preferred_element_type=jnp.float32
    )


def body(tokens, gate_weight, up_weight, down_weight, gate_mask, up_mask, down_mask, out_grad):
    feat = tokens.shape[1]
    both_all = lax.all_gather(
        jnp.concatenate([tokens, out_grad], axis=1), "col", axis=0, tiled=True
    )
    tok_all = both_all[:, :feat]
    grad_all = both_all[:, feat:]
    width = gate_weight.shape[1]
    tile = width // gate_mask.shape[1]
    tiles = gate_mask.shape[1]
    bounds = [tiles * k // CHUNKS for k in range(CHUNKS + 1)]

    gate_parts, up_parts, down_parts = [], [], []
    mixed_part = None
    input_part = None
    for k in range(CHUNKS):
        t0, t1 = bounds[k], bounds[k + 1]
        h0, h1 = t0 * tile, t1 * tile
        g_mask = gate_mask[:, t0:t1]
        u_mask = up_mask[:, t0:t1]
        d_mask = down_mask[t0:t1, :]
        w_gate = expand_flat(gate_weight[:, h0:h1], g_mask)
        w_up = expand_flat(up_weight[:, h0:h1], u_mask)
        w_down = expand_flat(down_weight[h0:h1, :], d_mask)
        n = h1 - h0
        gate_val, up_val = lax.psum(
            (
                jnp.dot(tok_all, w_gate, preferred_element_type=jnp.float32),
                jnp.dot(tok_all, w_up, preferred_element_type=jnp.float32),
            ),
            "row",
        )
        hg_part = contract_last(grad_all, w_down)
        ways = lax.axis_size("row")
        rows_all = hg_part.shape[0]
        hg_spread = lax.all_to_all(hg_part, "row", 0, 0, tiled=True)
        hg_mine = hg_spread.reshape(ways, rows_all // ways, n).sum(axis=0)
        hg_rep = jnp.broadcast_to(hg_mine[None], (ways, rows_all // ways, n)).reshape(rows_all, n)
        hidden_grad = lax.all_to_all(hg_rep, "row", 0, 0, tiled=True)
        sigmoid_gate = jax.nn.sigmoid(gate_val)
        silu_gate = gate_val * sigmoid_gate
        hidden = (silu_gate * up_val).astype(jnp.bfloat16)
        gate_grad = (
            hidden_grad * up_val * sigmoid_gate * (1.0 + gate_val * (1.0 - sigmoid_gate))
        ).astype(jnp.bfloat16)
        up_grad = (hidden_grad * silu_gate).astype(jnp.bfloat16)
        gate_parts.append(expand_flat(contract_first(tok_all, gate_grad), g_mask).astype(jnp.bfloat16))
        up_parts.append(expand_flat(contract_first(tok_all, up_grad), u_mask).astype(jnp.bfloat16))
        down_parts.append(expand_flat(contract_first(hidden, grad_all), d_mask).astype(jnp.bfloat16))
        m = jnp.dot(hidden, w_down, preferred_element_type=jnp.float32)
        i = contract_last(gate_grad, w_gate) + contract_last(up_grad, w_up)
        mixed_part = m if mixed_part is None else mixed_part + m
        input_part = i if input_part is None else input_part + i

    both_part = jnp.concatenate([mixed_part, input_part], axis=1)
    ways = lax.axis_size("col")
    spread = lax.all_to_all(both_part, "col", 0, 0, tiled=True)
    out_sums = spread.reshape(ways, spread.shape[0] // ways, spread.shape[1]).sum(axis=0)
    mixed_out = out_sums[:, :feat].astype(jnp.bfloat16)
    input_grad = out_sums[:, feat:].astype(jnp.bfloat16)
    grad_gate = jnp.concatenate(gate_parts, axis=1)
    grad_up = jnp.concatenate(up_parts, axis=1)
    grad_down = jnp.concatenate(down_parts, axis=0)
    return (mixed_out, grad_gate, grad_up, grad_down, input_grad)


def solution(mesh):
    in_specs = (
        P("col", "row"),
        P("row", "col"),
        P("row", "col"),
        P("col", "row"),
        P("row", "col"),
        P("row", "col"),
        P("col", "row"),
        P("col", "row"),
    )
    out_specs = (
        P("col", "row"),
        P("row", "col"),
        P("row", "col"),
        P("col", "row"),
        P("col", "row"),
    )
    return jax.shard_map(body, mesh=mesh, in_specs=in_specs, out_specs=out_specs, check_vma=False)
```

```python
import jax
import jax.numpy as jnp
from jax import lax
from jax.sharding import PartitionSpec as P

CHUNKS = 1


def expand(weight, mask):
    rows_w, cols_w = weight.shape
    tile_size = rows_w // mask.shape[0]
    blocks = weight.reshape(mask.shape[0], tile_size, mask.shape[1], tile_size)
    kept = mask.astype(weight.dtype)[:, None, :, None]
    return (blocks * kept).reshape(rows_w, cols_w)


def expand_flat(values, mask):
    rows_v, cols_v = values.shape
    rep_r = rows_v // mask.shape[0]
    rep_c = cols_v // mask.shape[1]
    kept = jnp.repeat(mask.astype(values.dtype), rep_c, axis=1)
    blocks = values.reshape(mask.shape[0], rep_r, cols_v)
    return (blocks * kept[:, None, :]).reshape(rows_v, cols_v)


def contract_last(left, right):
    return lax.dot_general(
        left, right, (((1,), (1,)), ((), ())), preferred_element_type=jnp.float32
    )


def contract_first(left, right):
    return lax.dot_general(
        left, right, (((0,), (0,)), ((), ())), preferred_element_type=jnp.float32
    )


def body(tokens, gate_weight, up_weight, down_weight, gate_mask, up_mask, down_mask, out_grad):
    feat = tokens.shape[1]
    both = jnp.concatenate([tokens, out_grad], axis=1)
    peers = lax.axis_size("col")
    both_rep = jnp.broadcast_to(both[None], (peers,) + both.shape).reshape(
        peers * both.shape[0], both.shape[1]
    )
    both_all = lax.all_to_all(both_rep, "col", 0, 0, tiled=True)
    tok_all = both_all[:, :feat]
    grad_all = both_all[:, feat:]
    width = gate_weight.shape[1]
    tile = width // gate_mask.shape[1]
    tiles = gate_mask.shape[1]
    bounds = [tiles * k // CHUNKS for k in range(CHUNKS + 1)]

    gate_parts, up_parts, down_parts = [], [], []
    mixed_part = None
    input_part = None
    prev_sums = None
    for k in range(CHUNKS):
        t0, t1 = bounds[k], bounds[k + 1]
        h0, h1 = t0 * tile, t1 * tile
        g_mask = gate_mask[:, t0:t1]
        u_mask = up_mask[:, t0:t1]
        d_mask = down_mask[t0:t1, :]
        w_gate = expand_flat(gate_weight[:, h0:h1], g_mask)
        w_up = expand_flat(up_weight[:, h0:h1], u_mask)
        w_down = expand_flat(down_weight[h0:h1, :], d_mask)
        n = h1 - h0
        partial = (
            jnp.dot(tok_all, w_gate, preferred_element_type=jnp.float32),
            jnp.dot(tok_all, w_up, preferred_element_type=jnp.float32),
            contract_last(grad_all, w_down),
        )
        if prev_sums is not None:
            partial, _ = lax.optimization_barrier((partial, prev_sums))
        gate_val, up_val, hidden_grad = lax.psum(partial, "row")
        prev_sums = gate_val
        sigmoid_gate = jax.nn.sigmoid(gate_val)
        silu_gate = gate_val * sigmoid_gate
        hidden = (silu_gate * up_val).astype(jnp.bfloat16)
        gate_grad = (
            hidden_grad * up_val * sigmoid_gate * (1.0 + gate_val * (1.0 - sigmoid_gate))
        ).astype(jnp.bfloat16)
        up_grad = (hidden_grad * silu_gate).astype(jnp.bfloat16)
        gate_parts.append(expand_flat(contract_first(tok_all, gate_grad), g_mask).astype(jnp.bfloat16))
        up_parts.append(expand_flat(contract_first(tok_all, up_grad), u_mask).astype(jnp.bfloat16))
        down_parts.append(expand_flat(contract_first(hidden, grad_all), d_mask).astype(jnp.bfloat16))
        m = jnp.dot(hidden, w_down, preferred_element_type=jnp.float32)
        i = contract_last(gate_grad, w_gate) + contract_last(up_grad, w_up)
        mixed_part = m if mixed_part is None else mixed_part + m
        input_part = i if input_part is None else input_part + i

    both_part = jnp.concatenate([mixed_part, input_part], axis=1)
    ways = lax.axis_size("col")
    spread = lax.all_to_all(both_part, "col", 0, 0, tiled=True)
    out_sums = spread.reshape(ways, spread.shape[0] // ways, spread.shape[1]).sum(axis=0)
    mixed_out = out_sums[:, :feat].astype(jnp.bfloat16)
    input_grad = out_sums[:, feat:].astype(jnp.bfloat16)
    grad_gate = jnp.concatenate(gate_parts, axis=1)
    grad_up = jnp.concatenate(up_parts, axis=1)
    grad_down = jnp.concatenate(down_parts, axis=0)
    return (mixed_out, grad_gate, grad_up, grad_down, input_grad)


def solution(mesh):
    in_specs = (
        P("col", "row"),
        P("row", "col"),
        P("row", "col"),
        P("col", "row"),
        P("row", "col"),
        P("row", "col"),
        P("col", "row"),
        P("col", "row"),
    )
    out_specs = (
        P("col", "row"),
        P("row", "col"),
        P("row", "col"),
        P("col", "row"),
        P("col", "row"),
    )
    return jax.shard_map(body, mesh=mesh, in_specs=in_specs, out_specs=out_specs, check_vma=False)
```

```python
import jax
import jax.numpy as jnp
from jax import lax
from jax.sharding import PartitionSpec as P

CHUNKS = 1


def expand(weight, mask):
    rows_w, cols_w = weight.shape
    tile_size = rows_w // mask.shape[0]
    blocks = weight.reshape(mask.shape[0], tile_size, mask.shape[1], tile_size)
    kept = mask.astype(weight.dtype)[:, None, :, None]
    return (blocks * kept).reshape(rows_w, cols_w)


def expand_flat(values, mask):
    rows_v, cols_v = values.shape
    rep_r = rows_v // mask.shape[0]
    rep_c = cols_v // mask.shape[1]
    kept = jnp.repeat(mask.astype(values.dtype), rep_c, axis=1)
    blocks = values.reshape(mask.shape[0], rep_r, cols_v)
    return (blocks * kept[:, None, :]).reshape(rows_v, cols_v)


def contract_last(left, right):
    return lax.dot_general(
        left, right, (((1,), (1,)), ((), ())), preferred_element_type=jnp.float32
    )


def contract_first(left, right):
    return lax.dot_general(
        left, right, (((0,), (0,)), ((), ())), preferred_element_type=jnp.float32
    )


def body(tokens, gate_weight, up_weight, down_weight, gate_mask, up_mask, down_mask, out_grad):
    feat = tokens.shape[1]
    both = jnp.concatenate([tokens, out_grad], axis=1)
    peers = lax.axis_size("col")
    both_rep = jnp.broadcast_to(both[None], (peers,) + both.shape).reshape(
        peers * both.shape[0], both.shape[1]
    )
    both_all = lax.all_to_all(both_rep, "col", 0, 0, tiled=True)
    tok_all = both_all[:, :feat]
    grad_all = both_all[:, feat:]
    width = gate_weight.shape[1]
    tile = width // gate_mask.shape[1]
    tiles = gate_mask.shape[1]
    bounds = [tiles * k // CHUNKS for k in range(CHUNKS + 1)]

    gate_parts, up_parts, down_parts = [], [], []
    mixed_part = None
    input_part = None
    prev_sums = None
    for k in range(CHUNKS):
        t0, t1 = bounds[k], bounds[k + 1]
        h0, h1 = t0 * tile, t1 * tile
        g_mask = gate_mask[:, t0:t1]
        u_mask = up_mask[:, t0:t1]
        d_mask = down_mask[t0:t1, :]
        w_gate = expand_flat(gate_weight[:, h0:h1], g_mask)
        w_up = expand_flat(up_weight[:, h0:h1], u_mask)
        w_down = expand_flat(down_weight[h0:h1, :], d_mask)
        n = h1 - h0
        partial = (
            jnp.dot(tok_all, w_gate, preferred_element_type=jnp.float32),
            jnp.dot(tok_all, w_up, preferred_element_type=jnp.float32),
            contract_last(grad_all, w_down),
        )
        if prev_sums is not None:
            partial, _ = lax.optimization_barrier((partial, prev_sums))
        gate_val, up_val, hidden_grad = lax.psum(partial, "row")
        prev_sums = gate_val
        sigmoid_gate = jax.nn.sigmoid(gate_val)
        silu_gate = gate_val * sigmoid_gate
        hidden = (silu_gate * up_val).astype(jnp.bfloat16)
        gate_grad = (
            hidden_grad * up_val * sigmoid_gate * (1.0 + gate_val * (1.0 - sigmoid_gate))
        ).astype(jnp.bfloat16)
        up_grad = (hidden_grad * silu_gate).astype(jnp.bfloat16)
        gate_parts.append(expand_flat(contract_first(tok_all, gate_grad), g_mask).astype(jnp.bfloat16))
        up_parts.append(expand_flat(contract_first(tok_all, up_grad), u_mask).astype(jnp.bfloat16))
        down_parts.append(expand_flat(contract_first(hidden, grad_all), d_mask).astype(jnp.bfloat16))
        m = jnp.dot(hidden, w_down, preferred_element_type=jnp.float32)
        i = contract_last(gate_grad, w_gate) + contract_last(up_grad, w_up)
        mixed_part = m if mixed_part is None else mixed_part + m
        input_part = i if input_part is None else input_part + i

    both_part = jnp.concatenate([mixed_part, input_part], axis=1)
    ways = lax.axis_size("col")
    spread = lax.all_to_all(both_part, "col", 0, 0, tiled=True)
    blocks = spread.reshape(ways, spread.shape[0] // ways, spread.shape[1])
    mixed_out = blocks[:, :, :feat].sum(axis=0).astype(jnp.bfloat16)
    input_grad = blocks[:, :, feat:].sum(axis=0).astype(jnp.bfloat16)
    grad_gate = jnp.concatenate(gate_parts, axis=1)
    grad_up = jnp.concatenate(up_parts, axis=1)
    grad_down = jnp.concatenate(down_parts, axis=0)
    return (mixed_out, grad_gate, grad_up, grad_down, input_grad)


def solution(mesh):
    in_specs = (
        P("col", "row"),
        P("row", "col"),
        P("row", "col"),
        P("col", "row"),
        P("row", "col"),
        P("row", "col"),
        P("col", "row"),
        P("col", "row"),
    )
    out_specs = (
        P("col", "row"),
        P("row", "col"),
        P("row", "col"),
        P("col", "row"),
        P("col", "row"),
    )
    return jax.shard_map(body, mesh=mesh, in_specs=in_specs, out_specs=out_specs, check_vma=False)
```

```python
import jax
import jax.numpy as jnp
from jax import lax
from jax.sharding import PartitionSpec as P

CHUNKS = 1


def expand(weight, mask):
    rows_w, cols_w = weight.shape
    tile_size = rows_w // mask.shape[0]
    blocks = weight.reshape(mask.shape[0], tile_size, mask.shape[1], tile_size)
    kept = mask.astype(weight.dtype)[:, None, :, None]
    return (blocks * kept).reshape(rows_w, cols_w)


def expand_flat(values, mask):
    rows_v, cols_v = values.shape
    rep_r = rows_v // mask.shape[0]
    rep_c = cols_v // mask.shape[1]
    kept = jnp.repeat(mask.astype(values.dtype), rep_c, axis=1)
    blocks = values.reshape(mask.shape[0], rep_r, cols_v)
    return (blocks * kept[:, None, :]).reshape(rows_v, cols_v)


def contract_last(left, right):
    return lax.dot_general(
        left, right, (((1,), (1,)), ((), ())), preferred_element_type=jnp.float32
    )


def contract_first(left, right):
    return lax.dot_general(
        left, right, (((0,), (0,)), ((), ())), preferred_element_type=jnp.float32
    )


def body(tokens, gate_weight, up_weight, down_weight, gate_mask, up_mask, down_mask, out_grad):
    feat = tokens.shape[1]
    both = jnp.concatenate([tokens, out_grad], axis=1)
    peers = lax.axis_size("col")
    both_rep = jnp.broadcast_to(both[None], (peers,) + both.shape).reshape(
        peers * both.shape[0], both.shape[1]
    )
    both_all = lax.all_to_all(both_rep, "col", 0, 0, tiled=True)
    tok_all = both_all[:, :feat]
    grad_all = both_all[:, feat:]
    width = gate_weight.shape[1]
    tile = width // gate_mask.shape[1]
    tiles = gate_mask.shape[1]
    bounds = [tiles * k // CHUNKS for k in range(CHUNKS + 1)]

    gate_parts, up_parts, down_parts = [], [], []
    mixed_part = None
    input_part = None
    for k in range(CHUNKS):
        t0, t1 = bounds[k], bounds[k + 1]
        h0, h1 = t0 * tile, t1 * tile
        g_mask = gate_mask[:, t0:t1]
        u_mask = up_mask[:, t0:t1]
        d_mask = down_mask[t0:t1, :]
        w_gate = expand_flat(gate_weight[:, h0:h1], g_mask)
        w_up = expand_flat(up_weight[:, h0:h1], u_mask)
        w_down = expand_flat(down_weight[h0:h1, :], d_mask)
        n = h1 - h0
        w_pair = jnp.concatenate([w_gate, w_up], axis=1)
        pair_val, hidden_grad = lax.psum(
            (
                jnp.dot(tok_all, w_pair, preferred_element_type=jnp.float32),
                contract_last(grad_all, w_down),
            ),
            "row",
        )
        gate_val = pair_val[:, :n]
        up_val = pair_val[:, n:]
        sigmoid_gate = jax.nn.sigmoid(gate_val)
        silu_gate = gate_val * sigmoid_gate
        hidden = (silu_gate * up_val).astype(jnp.bfloat16)
        gate_grad = (
            hidden_grad * up_val * sigmoid_gate * (1.0 + gate_val * (1.0 - sigmoid_gate))
        ).astype(jnp.bfloat16)
        up_grad = (hidden_grad * silu_gate).astype(jnp.bfloat16)
        gate_parts.append(expand_flat(contract_first(tok_all, gate_grad), g_mask).astype(jnp.bfloat16))
        up_parts.append(expand_flat(contract_first(tok_all, up_grad), u_mask).astype(jnp.bfloat16))
        down_parts.append(expand_flat(contract_first(hidden, grad_all), d_mask).astype(jnp.bfloat16))
        m = jnp.dot(hidden, w_down, preferred_element_type=jnp.float32)
        i = contract_last(gate_grad, w_gate) + contract_last(up_grad, w_up)
        mixed_part = m if mixed_part is None else mixed_part + m
        input_part = i if input_part is None else input_part + i

    both_part = jnp.concatenate([mixed_part, input_part], axis=1)
    ways = lax.axis_size("col")
    spread = lax.all_to_all(both_part, "col", 0, 0, tiled=True)
    out_sums = spread.reshape(ways, spread.shape[0] // ways, spread.shape[1]).sum(axis=0)
    mixed_out = out_sums[:, :feat].astype(jnp.bfloat16)
    input_grad = out_sums[:, feat:].astype(jnp.bfloat16)
    grad_gate = jnp.concatenate(gate_parts, axis=1)
    grad_up = jnp.concatenate(up_parts, axis=1)
    grad_down = jnp.concatenate(down_parts, axis=0)
    return (mixed_out, grad_gate, grad_up, grad_down, input_grad)


def solution(mesh):
    in_specs = (
        P("col", "row"),
        P("row", "col"),
        P("row", "col"),
        P("col", "row"),
        P("row", "col"),
        P("row", "col"),
        P("col", "row"),
        P("col", "row"),
    )
    out_specs = (
        P("col", "row"),
        P("row", "col"),
        P("row", "col"),
        P("col", "row"),
        P("col", "row"),
    )
    return jax.shard_map(body, mesh=mesh, in_specs=in_specs, out_specs=out_specs, check_vma=False)
```

```python
import jax
import jax.numpy as jnp
from jax import lax
from jax.sharding import PartitionSpec as P

CHUNKS = 1


def expand(weight, mask):
    rows_w, cols_w = weight.shape
    tile_size = rows_w // mask.shape[0]
    blocks = weight.reshape(mask.shape[0], tile_size, mask.shape[1], tile_size)
    kept = mask.astype(weight.dtype)[:, None, :, None]
    return (blocks * kept).reshape(rows_w, cols_w)


def expand_flat(values, mask):
    rows_v, cols_v = values.shape
    rep_r = rows_v // mask.shape[0]
    rep_c = cols_v // mask.shape[1]
    kept = jnp.repeat(mask.astype(values.dtype), rep_c, axis=1)
    blocks = values.reshape(mask.shape[0], rep_r, cols_v)
    return (blocks * kept[:, None, :]).reshape(rows_v, cols_v)


def contract_last(left, right):
    return lax.dot_general(
        left, right, (((1,), (1,)), ((), ())), preferred_element_type=jnp.float32
    )


def contract_first(left, right):
    return lax.dot_general(
        left, right, (((0,), (0,)), ((), ())), preferred_element_type=jnp.float32
    )


def body(tokens, gate_weight, up_weight, down_weight, gate_mask, up_mask, down_mask, out_grad):
    feat = tokens.shape[1]
    both = jnp.concatenate([tokens, out_grad], axis=1)
    peers = lax.axis_size("col")
    both_rep = jnp.broadcast_to(both[None], (peers,) + both.shape).reshape(
        peers * both.shape[0], both.shape[1]
    )
    both_all = lax.all_to_all(both_rep, "col", 0, 0, tiled=True)
    tok_all = both_all[:, :feat]
    grad_all = both_all[:, feat:]
    width = gate_weight.shape[1]
    tile = width // gate_mask.shape[1]
    tiles = gate_mask.shape[1]
    bounds = [tiles * k // CHUNKS for k in range(CHUNKS + 1)]

    gate_parts, up_parts, down_parts = [], [], []
    mixed_part = None
    input_part = None
    for k in range(CHUNKS):
        t0, t1 = bounds[k], bounds[k + 1]
        h0, h1 = t0 * tile, t1 * tile
        g_mask = gate_mask[:, t0:t1]
        u_mask = up_mask[:, t0:t1]
        d_mask = down_mask[t0:t1, :]
        w_gate = expand_flat(gate_weight[:, h0:h1], g_mask)
        w_up = expand_flat(up_weight[:, h0:h1], u_mask)
        w_down = expand_flat(down_weight[h0:h1, :], d_mask)
        n = h1 - h0
        w_pair = jnp.concatenate([w_gate, w_up], axis=1)
        pair_val, hidden_grad = lax.psum(
            (
                jnp.dot(tok_all, w_pair, preferred_element_type=jnp.float32),
                contract_last(grad_all, w_down),
            ),
            "row",
        )
        gate_val = pair_val[:, :n]
        up_val = pair_val[:, n:]
        sigmoid_gate = jax.nn.sigmoid(gate_val)
        silu_gate = gate_val * sigmoid_gate
        hidden = (silu_gate * up_val).astype(jnp.bfloat16)
        gate_grad = (
            hidden_grad * up_val * sigmoid_gate * (1.0 + gate_val * (1.0 - sigmoid_gate))
        ).astype(jnp.bfloat16)
        up_grad = (hidden_grad * silu_gate).astype(jnp.bfloat16)
        gate_parts.append(expand_flat(contract_first(tok_all, gate_grad), g_mask).astype(jnp.bfloat16))
        up_parts.append(expand_flat(contract_first(tok_all, up_grad), u_mask).astype(jnp.bfloat16))
        down_parts.append(expand_flat(contract_first(hidden, grad_all), d_mask).astype(jnp.bfloat16))
        m = jnp.dot(hidden, w_down, preferred_element_type=jnp.float32)
        i = contract_last(jnp.concatenate([gate_grad, up_grad], axis=1), w_pair)
        mixed_part = m if mixed_part is None else mixed_part + m
        input_part = i if input_part is None else input_part + i

    both_part = jnp.concatenate([mixed_part, input_part], axis=1)
    ways = lax.axis_size("col")
    spread = lax.all_to_all(both_part, "col", 0, 0, tiled=True)
    out_sums = spread.reshape(ways, spread.shape[0] // ways, spread.shape[1]).sum(axis=0)
    mixed_out = out_sums[:, :feat].astype(jnp.bfloat16)
    input_grad = out_sums[:, feat:].astype(jnp.bfloat16)
    grad_gate = jnp.concatenate(gate_parts, axis=1)
    grad_up = jnp.concatenate(up_parts, axis=1)
    grad_down = jnp.concatenate(down_parts, axis=0)
    return (mixed_out, grad_gate, grad_up, grad_down, input_grad)


def solution(mesh):
    in_specs = (
        P("col", "row"),
        P("row", "col"),
        P("row", "col"),
        P("col", "row"),
        P("row", "col"),
        P("row", "col"),
        P("col", "row"),
        P("col", "row"),
    )
    out_specs = (
        P("col", "row"),
        P("row", "col"),
        P("row", "col"),
        P("col", "row"),
        P("col", "row"),
    )
    return jax.shard_map(body, mesh=mesh, in_specs=in_specs, out_specs=out_specs, check_vma=False)
```
